256 devices in a mesh: ctx: 16 (over y_hi, z), head: 16 (over y_lo, x, core).
Axes of the slice: x: 4, y: 4 (y_hi: 2, y_lo: 2; y = y_hi * 2 + y_lo), z: 8, core: 2. Of those that a mesh axis runs over, the one named last changes fastest.
Arguments:
- hidden_rows: bfloat16 [2, 2048, 8192], P(None, 'ctx', 'head'), may hold values from -6 to 6
- w_qkv: bfloat16 [8, 8192, 768], P(None, 'head'), may hold values from -0.0625 to 0.0625
- kv_pool: bfloat16 [16, 512, 128, 256], P('head', 'ctx'), may hold values from -400 to 400
- page_home: int32 [2, 256, 1], replicated, may hold values from 0 to 15; in each aligned block of 16 rows (0 to 15, 16 to 31, ..., all dimensions but the last counted through in order) at most 2 rows name the same one
- recompute_idx: int32 [2, 2048], replicated, may hold values from 0 to 2047, as said below
- doc_lengths: int32 [2, 8], replicated, may hold values from 1 to 8192, 32768 in all within a row
Outputs:
- attn_out: bfloat16 [16, 2048, 512], P('head', 'ctx')
- kv_block: bfloat16 [16, 32768, 256], P('head', 'ctx')
The draws below stay inside these ranges and needn't reach their ends.
Inputs may be any that keep to these rules, and one draw needn't show every extreme that they name: `page_home`: in each aligned block of 16 pages (the pages of one block of tokens) at most 2 name the same pool device. `recompute_idx`: each aligned block of 128 entries holds distinct ascending positions, the first 0 and the last 2047. `doc_lengths`: each row sums to 32768.
All inputs are finite; a program needn't handle non-finite values.
Results may differ from the reference program's by a relative error of at most 0.035.
The reference program's roundings to bfloat16 on the way (of `queries`, `fresh_keys`, `fresh_values`, `fetched`, `cached_keys` and `weights`) count: a program that leaves them out, or rounds other values in their place, can miss the bound.
Values may be sent and summed in bfloat16 or wider, within the bound.
No kernel may reach another device: no remote copies, remote signals or barrier semaphores. Data moves between devices by JAX's collectives and lax.ppermute only.
A program may use at most 128 MiB of HBM per device.

```python
import math
import jax
import jax.numpy as jnp
import numpy as np
from jax import lax

D = 8192
HD = 128
KVH = 8
QG = 4
REQ = 2
PAGE = 128
CAP = 2
NDOC = 8
S_DEV = 2048
R = 128
C = 768
PAGES_DEV = 16
L = 32768
RT = 2048
PAGES = 256
N_CTX = 16


def draw_kv_pool(key, part):
    shape = (REQ * KVH, CAP * N_CTX * N_CTX, PAGE, 2 * HD)
    base_key = jax.random.fold_in(jax.random.fold_in(key, 11), 0)
    return jnp.clip(jax.random.normal(base_key, shape, jnp.float32), -6.0, 6.0).astype(jnp.bfloat16)


def draw_recompute_idx(key, part):
    block_keys = jax.random.split(jax.random.fold_in(key, 23), REQ * N_CTX)

    def one_block(block_key):
        inside_pick = jax.random.permutation(block_key, S_DEV - 2)[:R - 2].astype(jnp.int32) + 1
        picked = jnp.concatenate([jnp.zeros((1,), jnp.int32), inside_pick, jnp.full((1,), S_DEV - 1, jnp.int32)])
        return jnp.sort(picked)
    return jax.vmap(one_block)(block_keys).reshape(REQ, N_CTX * R).astype(jnp.int32)


def block_scale(own_key, extent, cuts, low, high):
    loudness, own = 1.0, jax.random.fold_in(own_key, 6)
    for dim, blocks in cuts:
        heights = jnp.exp(jax.random.uniform(jax.random.fold_in(own, dim), (blocks,), jnp.float32, low / len(cuts), high / len(cuts)))
        loudness = loudness * jnp.repeat(heights, extent[dim] // blocks).reshape([-1 if axis == dim else 1 for axis in range(len(extent))])
    return loudness


def split_up(count, total, most, lean):
    portions = [(1 << 20) // math.isqrt(standing ** lean) + 1 for standing in range(2, count + 1)]
    spare, given = total - most - (count - 1), [1] * (count - 1)
    while spare > 0:
        movable = [i for i in range(count - 1) if given[i] < most]
        mass, left = sum([portions[i] for i in movable]), spare
        for i in movable:
            extra = min(most - given[i], max(1, left * portions[i] // mass), spare)
            given[i] = given[i] + extra
            spare = spare - extra
    return np.array([most] + given)


def uneven(rng, number_of, total, bound, slope):
    if number_of == 2:
        one = jax.random.randint(rng, (), max(1, total - bound), min(bound, total - 1) + 1)
        return jnp.stack([one, total - one])
    tallies = jnp.asarray(split_up(number_of, total, bound, slope), jnp.int32)
    twos = (number_of - 1) // 2
    source_of, taker = tallies[1:1 + 2 * twos:2], tallies[2:2 + 2 * twos:2]
    margin = jnp.minimum(source_of - 1, bound - taker)
    passed = jax.random.randint(jax.random.fold_in(rng, 1), (twos,), 0, 1 << 20) % (margin + 1)
    tallies = tallies.at[1:1 + 2 * twos:2].set(source_of - passed).at[2:2 + 2 * twos:2].set(taker + passed)
    return tallies[jax.random.permutation(jax.random.fold_in(rng, 2), number_of)]


def assign_block(own_key, own, number, rows, count, top, reach, lean):
    sequence = jax.random.permutation(own_key, count)
    heavy_load, usual = shares(count, rows * top, reach, lean, True), shares(count, rows * top, reach, lean, False)
    places = jnp.arange(count)

    def named(sizes, rotation):
        used = int((sizes > 0).sum())
        fixed = max(1, used // 4)
        passed = fixed + (places - fixed + rotation * (used - fixed)) % max(1, count - fixed)
        return jnp.zeros((count,), jnp.int32).at[sequence[jnp.where(places < fixed, places, passed)]].set(jnp.asarray(sizes, jnp.int32))

    sizes = jnp.where(number % 4 == 0, named(heavy_load, number // 4), named(usual, number - number // 4 - 1))
    mixed = jax.random.permutation(jax.random.fold_in(own, 3), count)
    source_of, sink = mixed[0:count // 2 * 2:2], mixed[1:count // 2 * 2:2]
    room = jnp.minimum(sizes[source_of] - 1, reach - sizes[sink]) // 2
    room = jnp.where((source_of == sequence[0]) | (sink == sequence[0]) | (sizes[sink] == 0), 0, jnp.maximum(room, 0))
    passed = jax.random.randint(jax.random.fold_in(own, 4), (count // 2,), 0, 1 << 20) % (room + 1)
    sizes = sizes.at[source_of].add(-passed).at[sink].add(passed)
    items = jnp.searchsorted(jnp.cumsum(sizes), jnp.arange(rows * top), side="right").astype(jnp.int32)
    listing = items.reshape(top, rows).T
    listing = listing[jax.random.permutation(jax.random.fold_in(own, 1), rows)]
    rotation = jax.random.randint(jax.random.fold_in(own, 2), (rows, 1), 0, top)
    return jnp.take_along_axis(listing, (jnp.arange(top)[None, :] + rotation) % top, axis=1)


def shares(amount, total, limit, slope, full):
    loads = [(1 << 20) // math.isqrt(grade ** slope) + 1 for grade in range(1, amount + 1)]
    largest = limit if full else min(limit, max(-(-total // amount), total * loads[0] // sum(loads)))
    least = 1 if total - largest >= amount - 1 else 0
    counts, spare = [largest] + [least] * (amount - 1), total - largest - least * (amount - 1)
    while spare > 0:
        movable = [i for i in range(1, amount) if counts[i] < largest] or [i for i in range(1, amount) if counts[i] < limit]
        whole, budget = sum([loads[i] for i in movable]), spare
        for i in movable:
            addition = min(limit - counts[i], max(1, budget * loads[i] // whole), spare)
            counts[i] = counts[i] + addition
            spare = spare - addition
    return np.array(counts)


def bell_draw(stream_key, shape, deviation, reach, shards=(), held_as=jnp.bfloat16):
    level = block_scale(stream_key, shape, shards, -0.22, 0.18) if shards else 1.0
    result = jax.random.normal(stream_key, shape, jnp.float32) * deviation * level
    return jnp.minimum(jnp.maximum(result, -reach), reach).astype(held_as)


def setup_inputs(seed: int = 0) -> dict:
    seeds = jax.random.split(jax.random.key(seed), 7)
    hidden_rows = bell_draw(seeds[0], (REQ, RT, D), 1.0, 6.0, ((1, 16), (2, 16)))
    w_qkv = bell_draw(seeds[1], (KVH, D, C), D ** -0.5, 0.0625, ((1, 16),))
    kv_pool = draw_kv_pool(jax.random.fold_in(seeds[6], 71), 0)
    page_home_keys = jax.random.split(jax.random.fold_in(seeds[3], 1), REQ * PAGES // PAGES_DEV)
    page_home_turns = jax.random.permutation(jax.random.fold_in(seeds[3], 3), REQ * PAGES // PAGES_DEV)
    page_home = jax.vmap(lambda own, number: assign_block(jax.random.fold_in(seeds[3], 2), own, number, PAGES_DEV, N_CTX, 1, CAP, 2))(page_home_keys, page_home_turns).reshape((REQ, PAGES, 1))
    recompute_idx = draw_recompute_idx(jax.random.fold_in(seeds[6], 71), 0)
    doc_lengths = jax.vmap(lambda own: uneven(own, NDOC, L, L // 4, 2))(jax.random.split(seeds[5], REQ)).reshape((REQ, NDOC)).astype(jnp.int32)
    return dict(hidden_rows=hidden_rows, w_qkv=w_qkv, kv_pool=kv_pool, page_home=page_home, recompute_idx=recompute_idx, doc_lengths=doc_lengths)


blocked_score = -1e+30

def rope_tables(positions):
    half_dim = HD // 2
    inverse = jnp.exp(jnp.arange(half_dim, dtype=jnp.float32) * (-2.0 * math.log(500000.0) / HD))
    angles = positions.astype(jnp.float32)[:, None] * inverse[None, :]
    return (jnp.cos(angles), jnp.sin(angles))

def rotate(source, cosine, sine_part):
    half_dim = source.shape[-1] // 2
    leading = source[..., :half_dim]
    trailing = source[..., half_dim:]
    return jnp.concatenate([leading * cosine - trailing * sine_part, trailing * cosine + leading * sine_part], axis=-1)

def reference(hidden_rows, w_qkv, kv_pool, page_home, recompute_idx, doc_lengths):
    query_width = QG * HD
    score_scale = 1.0 / math.sqrt(HD)
    block_of_row = jnp.arange(N_CTX * R, dtype=jnp.int32) // R
    earlier = jnp.arange(PAGES_DEV)[:, None] > jnp.arange(PAGES_DEV)[None, :]
    owner_ids = jnp.arange(N_CTX, dtype=jnp.int32)[:, None]
    key_pos = jnp.arange(N_CTX * S_DEV, dtype=jnp.int32)
    outputs = []
    blocks = []
    for request in range(REQ):
        query_pos = (block_of_row * S_DEV + recompute_idx[request]).astype(jnp.int32)
        query_cos, query_sin = rope_tables(query_pos)
        home_dev = page_home[request, :, 0].reshape(N_CTX, PAGES_DEV)
        same_home = home_dev[:, :, None] == home_dev[:, None, :]
        page_rank = lax.optimization_barrier(jnp.sum(jnp.where(same_home & earlier[None], 1, 0), axis=2)).astype(jnp.int32)
        pool_index = (home_dev * (N_CTX * CAP) + owner_ids * CAP + page_rank).reshape(-1).astype(jnp.int32)
        doc_len = doc_lengths[request]
        doc_end = jnp.cumsum(doc_len)
        doc_offset = lax.optimization_barrier(jnp.sum(jnp.where(doc_end[None, :] <= key_pos[:, None], doc_len[None, :], 0), axis=1)).astype(jnp.int32)
        key_cos, key_sin = rope_tables(doc_offset)
        row_pos = jnp.repeat(query_pos, QG).reshape(N_CTX, R * QG)
        for kv_head in range(KVH):
            pair_id = request * KVH + kv_head
            projected = jnp.dot(hidden_rows[request].astype(jnp.float32), w_qkv[kv_head].astype(jnp.float32), precision=lax.Precision.HIGHEST, preferred_element_type=jnp.float32)
            queries = rotate(projected[:, :query_width].reshape(N_CTX * R, QG, HD), query_cos[:, None, :], query_sin[:, None, :]).astype(jnp.bfloat16)
            queries = lax.optimization_barrier(queries)
            fresh_keys = rotate(projected[:, query_width:query_width + HD], query_cos, query_sin).astype(jnp.bfloat16)
            fresh_values = projected[:, query_width + HD:].astype(jnp.bfloat16)
            fetched = kv_pool[pair_id][pool_index].reshape(N_CTX * S_DEV, 2 * HD)
            cached_keys = rotate(fetched[:, :HD].astype(jnp.float32), key_cos, key_sin).astype(jnp.bfloat16)
            new_block = jnp.concatenate([cached_keys, fetched[:, HD:]], axis=1)
            new_block = new_block.at[query_pos].set(jnp.concatenate([fresh_keys, fresh_values], axis=1))
            new_block = lax.optimization_barrier(new_block)
            keys_float = new_block[:, :HD].astype(jnp.float32)
            values_float = new_block[:, HD:].astype(jnp.float32)

            def attend(map_input):
                block_queries, block_pos = map_input
                scores = jnp.dot(block_queries.astype(jnp.float32), keys_float.T, precision=lax.Precision.HIGHEST, preferred_element_type=jnp.float32) * score_scale
                visible = key_pos[None, :] <= block_pos[:, None]
                masked = jnp.where(visible, scores, blocked_score)
                row_top = lax.optimization_barrier(jnp.max(masked, axis=1, keepdims=True))
                probs = jnp.where(visible, jnp.exp(masked - row_top), 0.0)
                weights = lax.optimization_barrier(probs.astype(jnp.bfloat16)).astype(jnp.float32)
                summed = jnp.dot(weights, values_float, precision=lax.Precision.HIGHEST, preferred_element_type=jnp.float32)
                return (summed / lax.optimization_barrier(jnp.sum(probs, axis=1, keepdims=True))).astype(jnp.bfloat16)
            attended = lax.map(attend, (queries.reshape(N_CTX, R * QG, HD), row_pos))
            outputs.append(attended.reshape(N_CTX * R, query_width))
            blocks.append(new_block)
    return (jnp.stack(outputs), jnp.stack(blocks))
```

```python
import functools
import math

import jax
import jax.numpy as jnp
from jax import lax
from jax.experimental import pallas as pl
from jax.experimental.pallas import tpu as pltpu
from jax.sharding import Mesh, PartitionSpec as P

HD = 128
KVH = 8
QG = 4
REQ = 2
PAGE = 128
CAP = 2
S_DEV = 2048
R = 128
NDOC = 8
PAGES_DEV = S_DEV // PAGE

YH, ZZ, YL, XX, CC = 2, 8, 2, 4, 2
CTX = ("yh", "z")
NCTX = YH * ZZ
HALF = QG // YH * R
TAIL = 16
LOG2E = 1.4426950408889634
SCALE2 = LOG2E / math.sqrt(HD)
EMPTY = -1e30
MIB = 1 << 20

bf16 = jnp.bfloat16
f32 = jnp.float32


def rope_tables(positions):
    half_dim = HD // 2
    inverse = jnp.exp(jnp.arange(half_dim, dtype=f32) * (-2.0 * math.log(500000.0) / HD))
    angles = positions.astype(f32)[:, None] * inverse[None, :]
    cosine, sine = jnp.cos(angles), jnp.sin(angles)
    return (jnp.concatenate([cosine, cosine], axis=1), jnp.concatenate([-sine, sine], axis=1))


def rotated(v, cosine, sine):
    return v * cosine + pltpu.roll(v, HD // 2, 1) * sine


def partial_send_kernel(core_ref, x_ref, w_ref, o_ref):
    acc = jnp.dot(x_ref[...], w_ref[0], preferred_element_type=f32)
    o_ref[:, 0] = acc.reshape(REQ, R, -1).astype(bf16)


def partial_keep_kernel(core_ref, x_ref, w_ref, r_ref, o_ref):
    acc = jnp.dot(x_ref[...], w_ref[0], preferred_element_type=f32)
    o_ref[:, 0] = (acc.reshape(REQ, R, -1) + r_ref[:, 0].astype(f32)).astype(bf16)


def partials(parity, x, w, received=None):
    d, c = w.shape[1:]
    block = pl.BlockSpec((REQ, 1, R, c), lambda i, core: (0, i, 0, 0))
    in_specs = [
        pl.BlockSpec((REQ * R, d), lambda i, core: (0, 0)),
        pl.BlockSpec((1, d, c), lambda i, core: (2 * i + core[0], 0, 0)),
    ]
    args = [parity, x, w]
    if received is not None:
        in_specs.append(block)
        args.append(received)
    return pl.pallas_call(
        partial_send_kernel if received is None else partial_keep_kernel,
        out_shape=jax.ShapeDtypeStruct((REQ, XX, R, c), bf16),
        grid_spec=pltpu.PrefetchScalarGridSpec(
            num_scalar_prefetch=1, grid=(XX,), in_specs=in_specs, out_specs=block
        ),
        compiler_params=pltpu.CompilerParams(vmem_limit_bytes=24 * MIB),
    )(*args)


def query_kernel(p_ref, cos_ref, sin_ref, q_ref, fresh_ref):
    col = pl.program_id(0)
    total = jnp.sum(p_ref[...].astype(f32), axis=0)

    @pl.when(col < QG)
    def _():
        q = rotated(total, cos_ref[...], sin_ref[...]).astype(bf16)
        for z in range(ZZ):
            q_ref[0, z] = q

    @pl.when(col == QG)
    def _():
        fresh_ref[...] = rotated(total, cos_ref[...], sin_ref[...]).astype(bf16)

    @pl.when(col == QG + 1)
    def _():
        fresh_ref[...] = total.astype(bf16)


def make_queries(pieces, cosine, sine):
    n = pieces.shape[0]
    return pl.pallas_call(
        query_kernel,
        out_shape=(
            jax.ShapeDtypeStruct((YH, ZZ, HALF, HD), bf16),
            jax.ShapeDtypeStruct((R, 2 * HD), bf16),
        ),
        grid=(QG + 2,),
        in_specs=[
            pl.BlockSpec((n, R, HD), lambda c: (0, 0, c)),
            pl.BlockSpec((R, HD), lambda c: (0, 0)),
            pl.BlockSpec((R, HD), lambda c: (0, 0)),
        ],
        out_specs=(
            pl.BlockSpec(
                (1, ZZ, R, HD),
                lambda c: (jnp.minimum(c, QG - 1) // 2, 0, jnp.minimum(c, QG - 1) % 2, 0),
            ),
            pl.BlockSpec((R, HD), lambda c: (0, jnp.maximum(c - QG, 0))),
        ),
        compiler_params=pltpu.CompilerParams(vmem_limit_bytes=24 * MIB),
    )(pieces, cosine, sine)


def kv_kernel(slot_ref, start_ref, page_ref, idx_ref, fresh_ref, cos_ref, sin_ref, o_ref):
    g = pl.program_id(0)
    row = lax.broadcasted_iota(jnp.int32, (PAGE, 1), 0) + g * PAGE
    cosine = jnp.broadcast_to(cos_ref[0:1, :], (PAGE, HD))
    sine = jnp.broadcast_to(sin_ref[0:1, :], (PAGE, HD))
    for d in range(1, NDOC):
        later = row >= start_ref[d]
        cosine = jnp.where(later, cos_ref[d : d + 1, :], cosine)
        sine = jnp.where(later, sin_ref[d : d + 1, :], sine)
    hit = idx_ref[...] == row
    fresh = jnp.dot(
        jnp.where(hit, 1.0, 0.0).astype(bf16), fresh_ref[...], preferred_element_type=f32
    )
    replaced = jnp.sum(jnp.where(hit, 1.0, 0.0), axis=1, keepdims=True) > 0.0
    keys = rotated(page_ref[0, :, :HD].astype(f32), cosine, sine)
    o_ref[:, :HD] = jnp.where(replaced, fresh[:, :HD], keys).astype(bf16)
    o_ref[:, HD:] = jnp.where(replaced, fresh[:, HD:], page_ref[0, :, HD:].astype(f32)).astype(bf16)


def build_block(slots, starts, pages, local_index, fresh, cosine, sine):
    return pl.pallas_call(
        kv_kernel,
        out_shape=jax.ShapeDtypeStruct((S_DEV, 2 * HD), bf16),
        grid_spec=pltpu.PrefetchScalarGridSpec(
            num_scalar_prefetch=2,
            grid=(PAGES_DEV,),
            in_specs=[
                pl.BlockSpec((1, PAGE, 2 * HD), lambda g, s, t: (s[g], 0, 0)),
                pl.BlockSpec((1, R), lambda g, s, t: (0, 0)),
                pl.BlockSpec((R, 2 * HD), lambda g, s, t: (0, 0)),
                pl.BlockSpec((NDOC, HD), lambda g, s, t: (0, 0)),
                pl.BlockSpec((NDOC, HD), lambda g, s, t: (0, 0)),
            ],
            out_specs=pl.BlockSpec((PAGE, 2 * HD), lambda g, s, t: (g, 0)),
        ),
    )(slots, starts, pages, local_index, fresh, cosine, sine)


def attend_kernel(block_ref, q_ref, own_ref, other_ref, pos_ref, o_ref, top_ref, acc_ref):
    c = pl.program_id(0)
    top_ref[...] = jnp.full((HALF, HD), EMPTY, f32)
    acc_ref[...] = jnp.zeros((HALF, 2 * HD), f32)

    def fold(kv_ref, masked):
        q = q_ref[0]
        chunk = 512
        pieces = []
        top = top_ref[:, 0:1]
        for k in range(S_DEV // chunk):
            keys = kv_ref[k * chunk : (k + 1) * chunk, :HD]
            s = lax.dot_general(q, keys, (((1,), (1,)), ((), ())), preferred_element_type=f32)
            if masked:
                key_pos = lax.broadcasted_iota(jnp.int32, (HALF, chunk), 1) + k * chunk
                s = jnp.where(key_pos <= pos_ref[0], s, EMPTY)
            pieces.append(s)
        best = functools.reduce(jnp.maximum, pieces)
        new_top = jnp.maximum(top, jnp.max(best, axis=1, keepdims=True))
        base = new_top * SCALE2
        total = acc_ref[...] * jnp.exp2(top * SCALE2 - base)
        ones = jnp.ones((chunk, HD), bf16)
        for k, s in enumerate(pieces):
            weights = jnp.exp2(s * SCALE2 - base).astype(bf16)
            values = jnp.concatenate([kv_ref[k * chunk : (k + 1) * chunk, HD:], ones], axis=1)
            total = total + jnp.dot(weights, values, preferred_element_type=f32)
        acc_ref[...] = total
        top_ref[...] = jnp.broadcast_to(new_top, (HALF, HD))

    for n, kv_ref in ((0, own_ref), (1, other_ref)):
        pl.when(c > block_ref[n])(functools.partial(fold, kv_ref, False))
        pl.when(c == block_ref[n])(functools.partial(fold, kv_ref, True))

    denominator = acc_ref[:, HD:]
    there = denominator > 0.0
    safe = jnp.where(there, denominator, 1.0)
    o_ref[0, :HALF] = (acc_ref[:, :HD] / safe).astype(bf16)
    lse = jnp.where(there, top_ref[...] * SCALE2 + jnp.log2(safe), EMPTY)
    place = lax.broadcasted_iota(jnp.int32, (TAIL, R), 0)
    tail = jnp.zeros((TAIL, R), f32)
    for n in range(HALF // R):
        rest = jnp.transpose(lse[n * R : (n + 1) * R])[:TAIL]
        for k in range(3):
            term = rest.astype(bf16).astype(f32)
            rest = rest - term
            tail = jnp.where(place == 3 * n + k, term, tail)
    o_ref[0, HALF:] = tail.astype(bf16)


def attend(blocks, queries, own, other, positions):
    return pl.pallas_call(
        attend_kernel,
        out_shape=jax.ShapeDtypeStruct((NCTX, HALF + TAIL, HD), bf16),
        grid_spec=pltpu.PrefetchScalarGridSpec(
            num_scalar_prefetch=1,
            grid=(NCTX,),
            in_specs=[
                pl.BlockSpec((1, HALF, HD), lambda c, b: (c, 0, 0)),
                pl.BlockSpec((S_DEV, 2 * HD), lambda c, b: (0, 0)),
                pl.BlockSpec((S_DEV, 2 * HD), lambda c, b: (0, 0)),
                pl.BlockSpec((1, HALF, 1), lambda c, b: (c, 0, 0)),
            ],
            out_specs=pl.BlockSpec((1, HALF + TAIL, HD), lambda c, b: (c, 0, 0)),
            scratch_shapes=[pltpu.VMEM((HALF, HD), f32), pltpu.VMEM((HALF, 2 * HD), f32)],
        ),
        compiler_params=pltpu.CompilerParams(vmem_limit_bytes=40 * MIB),
    )(blocks, queries, own, other, positions)


def merge_kernel(p_ref, o_ref):
    for n in range(HALF // R):
        lse = jnp.concatenate(
            [
                sum(p_ref[i, HALF + 3 * n + k : HALF + 3 * n + k + 1, :].astype(f32) for k in range(3))
                for i in range(ZZ)
            ],
            axis=0,
        )
        share = jnp.exp2(lse - jnp.max(lse, axis=0, keepdims=True))
        share = share / jnp.sum(share, axis=0, keepdims=True)
        columns = jnp.transpose(jnp.concatenate([share] * (R // ZZ), axis=0))
        total = sum(
            p_ref[i, n * R : (n + 1) * R, :].astype(f32) * columns[:, i : i + 1] for i in range(ZZ)
        )
        o_ref[:, n * HD : (n + 1) * HD] = total.astype(bf16)


def merge(parts):
    return pl.pallas_call(
        merge_kernel,
        out_shape=jax.ShapeDtypeStruct((R, QG * HD), bf16),
        grid=(YH,),
        in_specs=[pl.BlockSpec((ZZ, HALF + TAIL, HD), lambda y: (y, 0, 0))],
        out_specs=pl.BlockSpec((R, HALF // R * HD), lambda y: (0, y)),
        compiler_params=pltpu.CompilerParams(vmem_limit_bytes=24 * MIB),
    )(parts)


def per_device(hidden_rows, w_qkv, kv_pool, page_home, recompute_idx, doc_lengths):
    yh, z = lax.axis_index("yh"), lax.axis_index("z")
    request = lax.axis_index("yl")
    core = lax.axis_index("core")
    ctx_rank = yh * ZZ + z

    local = lax.dynamic_index_in_dim(recompute_idx.reshape(REQ, NCTX, R), request, 0, False)
    local_index = lax.dynamic_slice(local, (ctx_rank, 0), (1, R))
    query_cos, query_sin = rope_tables(ctx_rank * S_DEV + local_index[0])
    home_dev = lax.dynamic_slice(
        page_home, (request, ctx_rank * PAGES_DEV, 0), (1, PAGES_DEV, 1)
    ).reshape(PAGES_DEV)
    same_home = home_dev[:, None] == home_dev[None, :]
    earlier = jnp.arange(PAGES_DEV)[:, None] > jnp.arange(PAGES_DEV)[None, :]
    page_rank = jnp.sum(jnp.where(same_home & earlier, 1, 0), axis=1).astype(jnp.int32)
    slots = home_dev * CAP + page_rank
    doc_len = lax.dynamic_index_in_dim(doc_lengths, request, 0, keepdims=False)
    docs = jnp.arange(NDOC)
    doc_start = jnp.sum(jnp.where(docs[None, :] < docs[:, None], doc_len[None, :], 0), axis=1)
    doc_cos, doc_sin = rope_tables(doc_start)
    starts = (doc_start - ctx_rank * S_DEV).astype(jnp.int32)
    blocks = jnp.stack([ctx_rank, (1 - yh) * ZZ + z]).astype(jnp.int32)
    positions = jnp.concatenate([local, local], axis=1)[:, :, None]

    pages = lax.all_to_all(kv_pool[0], CTX, split_axis=0, concat_axis=0, tiled=True)

    x = hidden_rows.reshape(REQ * R, hidden_rows.shape[2])
    theirs = partials((1 - core).reshape(1).astype(jnp.int32), x, w_qkv)
    received = lax.ppermute(theirs, "core", [(0, 1), (1, 0)])
    mine = partials(core.reshape(1).astype(jnp.int32), x, w_qkv, received)
    pieces = lax.all_to_all(
        mine.reshape(REQ * XX, R, mine.shape[3]), ("yl", "x"), split_axis=0, concat_axis=0, tiled=True
    )
    queries, fresh = make_queries(pieces, query_cos, query_sin)
    queries = lax.all_to_all(
        queries.reshape(NCTX, HALF, HD), CTX, split_axis=0, concat_axis=0, tiled=True
    )

    own = build_block(slots, starts, pages, local_index, fresh, doc_cos, doc_sin)
    other = lax.ppermute(own, "yh", [(0, 1), (1, 0)])
    parts = attend(blocks, queries, own, other, positions)
    parts = lax.all_to_all(parts, CTX, split_axis=0, concat_axis=0, tiled=True)
    return (merge(parts)[None], own[None])


def solution(mesh):
    fine = Mesh(mesh.devices.reshape(YH, ZZ, YL, XX, CC), ("yh", "z", "yl", "x", "core"))
    head = ("yl", "x", "core")
    in_specs = (
        P(None, CTX, head),
        P(None, head, None),
        P(head, CTX, None, None),
        P(),
        P(),
        P(),
    )
    out_specs = (P(head, CTX, None), P(head, CTX, None))
    return jax.shard_map(
        per_device, mesh=fine, in_specs=in_specs, out_specs=out_specs, check_vma=False
    )
```

```python
import functools
import math

import jax
import jax.numpy as jnp
from jax import lax
from jax.experimental import pallas as pl
from jax.experimental.pallas import tpu as pltpu
from jax.sharding import Mesh, PartitionSpec as P

HD = 128
KVH = 8
QG = 4
REQ = 2
PAGE = 128
CAP = 2
S_DEV = 2048
R = 128
NDOC = 8
PAGES_DEV = S_DEV // PAGE

YH, ZZ, YL, XX, CC = 2, 8, 2, 4, 2
CTX = ("yh", "z")
NCTX = YH * ZZ
HALF = QG // YH * R
TAIL = 16
LOG2E = 1.4426950408889634
SCALE2 = LOG2E / math.sqrt(HD)
EMPTY = -1e30
MIB = 1 << 20

bf16 = jnp.bfloat16
f32 = jnp.float32


def rope_tables(positions):
    half_dim = HD // 2
    inverse = jnp.exp(jnp.arange(half_dim, dtype=f32) * (-2.0 * math.log(500000.0) / HD))
    angles = positions.astype(f32)[:, None] * inverse[None, :]
    cosine, sine = jnp.cos(angles), jnp.sin(angles)
    return (jnp.concatenate([cosine, cosine], axis=1), jnp.concatenate([-sine, sine], axis=1))


def rotated(v, cosine, sine):
    return v * cosine + pltpu.roll(v, HD // 2, 1) * sine


def partial_send_kernel(at_ref, x_ref, w_ref, o_ref):
    acc = jnp.dot(x_ref[...], w_ref[0], preferred_element_type=f32)
    for r in range(REQ):
        o_ref[r ^ at_ref[2], 0] = acc[r * R : (r + 1) * R].astype(bf16)


def partial_keep_kernel(at_ref, x_ref, w_ref, r_ref, o_ref):
    acc = jnp.dot(x_ref[...], w_ref[0], preferred_element_type=f32)
    for r in range(REQ):
        far = r ^ at_ref[2]
        o_ref[far, 0] = (acc[r * R : (r + 1) * R] + r_ref[far, 0].astype(f32)).astype(bf16)


def partials(place, x, w, received=None):
    d, c = w.shape[1:]
    block = pl.BlockSpec((REQ, 1, R, c), lambda i, at: (0, i ^ at[1], 0, 0))
    in_specs = [
        pl.BlockSpec((REQ * R, d), lambda i, at: (0, 0)),
        pl.BlockSpec((1, d, c), lambda i, at: (2 * i + at[0], 0, 0)),
    ]
    args = [place, x, w]
    if received is not None:
        in_specs.append(block)
        args.append(received)
    return pl.pallas_call(
        partial_send_kernel if received is None else partial_keep_kernel,
        out_shape=jax.ShapeDtypeStruct((REQ, XX, R, c), bf16),
        grid_spec=pltpu.PrefetchScalarGridSpec(
            num_scalar_prefetch=1, grid=(XX,), in_specs=in_specs, out_specs=block
        ),
        compiler_params=pltpu.CompilerParams(vmem_limit_bytes=24 * MIB),
    )(*args)


def query_kernel(*refs):
    *piece_refs, cos_ref, sin_ref, q_ref, fresh_ref = refs
    col = pl.program_id(0)
    total = sum(p_ref[...].astype(f32) for p_ref in piece_refs)

    @pl.when(col < QG)
    def _():
        q = rotated(total, cos_ref[...], sin_ref[...]).astype(bf16)
        for z in range(ZZ):
            q_ref[0, z] = q

    @pl.when(col == QG)
    def _():
        fresh_ref[...] = rotated(total, cos_ref[...], sin_ref[...]).astype(bf16)

    @pl.when(col == QG + 1)
    def _():
        fresh_ref[...] = total.astype(bf16)


def make_queries(pieces, cosine, sine):
    return pl.pallas_call(
        query_kernel,
        out_shape=(
            jax.ShapeDtypeStruct((YH, ZZ, HALF, HD), bf16),
            jax.ShapeDtypeStruct((R, 2 * HD), bf16),
        ),
        grid=(QG + 2,),
        in_specs=[
            *[pl.BlockSpec((R, HD), lambda c: (0, c))] * len(pieces),
            pl.BlockSpec((R, HD), lambda c: (0, 0)),
            pl.BlockSpec((R, HD), lambda c: (0, 0)),
        ],
        out_specs=(
            pl.BlockSpec(
                (1, ZZ, R, HD),
                lambda c: (jnp.minimum(c, QG - 1) // 2, 0, jnp.minimum(c, QG - 1) % 2, 0),
            ),
            pl.BlockSpec((R, HD), lambda c: (0, jnp.maximum(c - QG, 0))),
        ),
        compiler_params=pltpu.CompilerParams(vmem_limit_bytes=24 * MIB),
    )(*pieces, cosine, sine)


def kv_kernel(slot_ref, start_ref, page_ref, idx_ref, fresh_ref, cos_ref, sin_ref, o_ref, buf_ref, sem):
    copies = [
        pltpu.make_async_copy(page_ref.at[slot_ref[g]], buf_ref.at[g], sem.at[g])
        for g in range(PAGES_DEV)
    ]
    for copy in copies:
        copy.start()
    column = lax.broadcasted_iota(jnp.int32, (PAGE, 1), 0)
    for g, copy in enumerate(copies):
        row = column + g * PAGE
        cosine = jnp.broadcast_to(cos_ref[0:1, :], (PAGE, HD))
        sine = jnp.broadcast_to(sin_ref[0:1, :], (PAGE, HD))
        for d in range(1, NDOC):
            later = row >= start_ref[d]
            cosine = jnp.where(later, cos_ref[d : d + 1, :], cosine)
            sine = jnp.where(later, sin_ref[d : d + 1, :], sine)
        hit = jnp.where(idx_ref[...] == row, 1.0, 0.0)
        fresh = jnp.dot(hit.astype(bf16), fresh_ref[...], preferred_element_type=f32)
        replaced = jnp.sum(hit, axis=1, keepdims=True) > 0.0
        copy.wait()
        keys = rotated(buf_ref[g, :, :HD].astype(f32), cosine, sine)
        values = buf_ref[g, :, HD:].astype(f32)
        here = pl.ds(g * PAGE, PAGE)
        o_ref[here, :HD] = jnp.where(replaced, fresh[:, :HD], keys).astype(bf16)
        o_ref[here, HD:] = jnp.where(replaced, fresh[:, HD:], values).astype(bf16)


def build_block(slots, starts, pages, local_index, fresh, cosine, sine):
    whole = pl.BlockSpec(memory_space=pltpu.VMEM)
    return pl.pallas_call(
        kv_kernel,
        out_shape=jax.ShapeDtypeStruct((S_DEV, 2 * HD), bf16),
        grid_spec=pltpu.PrefetchScalarGridSpec(
            num_scalar_prefetch=2,
            grid=(),
            in_specs=[pl.BlockSpec(memory_space=pl.ANY), whole, whole, whole, whole],
            out_specs=whole,
            scratch_shapes=[
                pltpu.VMEM((PAGES_DEV, PAGE, 2 * HD), bf16),
                pltpu.SemaphoreType.DMA((PAGES_DEV,)),
            ],
        ),
        compiler_params=pltpu.CompilerParams(vmem_limit_bytes=24 * MIB),
    )(slots, starts, pages, local_index, fresh, cosine, sine)


def attend_kernel(block_ref, q_ref, own_ref, other_ref, pos_ref, o_ref, top_ref, acc_ref):
    c = pl.program_id(0)
    top_ref[...] = jnp.full((HALF, HD), EMPTY, f32)
    acc_ref[...] = jnp.zeros((HALF, 2 * HD), f32)

    def fold(kv_ref, masked):
        q = q_ref[0]
        chunk = 512
        pieces = []
        top = top_ref[:, 0:1]
        for k in range(S_DEV // chunk):
            keys = kv_ref[k * chunk : (k + 1) * chunk, :HD]
            s = lax.dot_general(q, keys, (((1,), (1,)), ((), ())), preferred_element_type=f32)
            if masked:
                key_pos = lax.broadcasted_iota(jnp.int32, (HALF, chunk), 1) + k * chunk
                s = jnp.where(key_pos <= pos_ref[0], s, EMPTY)
            pieces.append(s)
        best = functools.reduce(jnp.maximum, pieces)
        new_top = jnp.maximum(top, jnp.max(best, axis=1, keepdims=True))
        base = new_top * SCALE2
        total = acc_ref[...] * jnp.exp2(top * SCALE2 - base)
        ones = jnp.ones((chunk, HD), bf16)
        for k, s in enumerate(pieces):
            weights = jnp.exp2(s * SCALE2 - base).astype(bf16)
            values = jnp.concatenate([kv_ref[k * chunk : (k + 1) * chunk, HD:], ones], axis=1)
            total = total + jnp.dot(weights, values, preferred_element_type=f32)
        acc_ref[...] = total
        top_ref[...] = jnp.broadcast_to(new_top, (HALF, HD))

    for n, kv_ref in ((0, own_ref), (1, other_ref)):
        pl.when(c > block_ref[n])(functools.partial(fold, kv_ref, False))
        pl.when(c == block_ref[n])(functools.partial(fold, kv_ref, True))

    denominator = acc_ref[:, HD:]
    there = denominator > 0.0
    safe = jnp.where(there, denominator, 1.0)
    o_ref[0, :HALF] = (acc_ref[:, :HD] / safe).astype(bf16)
    lse = jnp.where(there, top_ref[...] * SCALE2 + jnp.log2(safe), EMPTY)
    place = lax.broadcasted_iota(jnp.int32, (TAIL, R), 0)
    tail = jnp.zeros((TAIL, R), f32)
    for n in range(HALF // R):
        rest = jnp.transpose(lse[n * R : (n + 1) * R])[:TAIL]
        for k in range(3):
            term = rest.astype(bf16).astype(f32)
            rest = rest - term
            tail = jnp.where(place == 3 * n + k, term, tail)
    o_ref[0, HALF:] = tail.astype(bf16)


def attend(blocks, queries, own, other, positions):
    return pl.pallas_call(
        attend_kernel,
        out_shape=jax.ShapeDtypeStruct((NCTX, HALF + TAIL, HD), bf16),
        grid_spec=pltpu.PrefetchScalarGridSpec(
            num_scalar_prefetch=1,
            grid=(NCTX,),
            in_specs=[
                pl.BlockSpec((1, HALF, HD), lambda c, b: (c, 0, 0)),
                pl.BlockSpec((S_DEV, 2 * HD), lambda c, b: (0, 0)),
                pl.BlockSpec((S_DEV, 2 * HD), lambda c, b: (0, 0)),
                pl.BlockSpec((1, HALF, 1), lambda c, b: (c, 0, 0)),
            ],
            out_specs=pl.BlockSpec((1, HALF + TAIL, HD), lambda c, b: (c, 0, 0)),
            scratch_shapes=[pltpu.VMEM((HALF, HD), f32), pltpu.VMEM((HALF, 2 * HD), f32)],
        ),
        compiler_params=pltpu.CompilerParams(vmem_limit_bytes=40 * MIB),
    )(blocks, queries, own, other, positions)


def merge_kernel(p_ref, o_ref):
    for n in range(HALF // R):
        lse = jnp.concatenate(
            [
                sum(p_ref[i, HALF + 3 * n + k : HALF + 3 * n + k + 1, :].astype(f32) for k in range(3))
                for i in range(ZZ)
            ],
            axis=0,
        )
        share = jnp.exp2(lse - jnp.max(lse, axis=0, keepdims=True))
        share = share / jnp.sum(share, axis=0, keepdims=True)
        columns = jnp.transpose(jnp.concatenate([share] * (R // ZZ), axis=0))
        total = sum(
            p_ref[i, n * R : (n + 1) * R, :].astype(f32) * columns[:, i : i + 1] for i in range(ZZ)
        )
        o_ref[:, n * HD : (n + 1) * HD] = total.astype(bf16)


def merge(parts):
    return pl.pallas_call(
        merge_kernel,
        out_shape=jax.ShapeDtypeStruct((R, QG * HD), bf16),
        grid=(YH,),
        in_specs=[pl.BlockSpec((ZZ, HALF + TAIL, HD), lambda y: (y, 0, 0))],
        out_specs=pl.BlockSpec((R, HALF // R * HD), lambda y: (0, y)),
        compiler_params=pltpu.CompilerParams(vmem_limit_bytes=24 * MIB),
    )(parts)


def per_device(hidden_rows, w_qkv, kv_pool, page_home, recompute_idx, doc_lengths):
    yh, z = lax.axis_index("yh"), lax.axis_index("z")
    request = lax.axis_index("yl")
    core = lax.axis_index("core")
    ctx_rank = yh * ZZ + z

    local = lax.dynamic_index_in_dim(recompute_idx.reshape(REQ, NCTX, R), request, 0, False)
    local_index = lax.dynamic_slice(local, (ctx_rank, 0), (1, R))
    query_cos, query_sin = rope_tables(ctx_rank * S_DEV + local_index[0])
    home_dev = lax.dynamic_slice(
        page_home, (request, ctx_rank * PAGES_DEV, 0), (1, PAGES_DEV, 1)
    ).reshape(PAGES_DEV)
    same_home = home_dev[:, None] == home_dev[None, :]
    earlier = jnp.arange(PAGES_DEV)[:, None] > jnp.arange(PAGES_DEV)[None, :]
    page_rank = jnp.sum(jnp.where(same_home & earlier, 1, 0), axis=1).astype(jnp.int32)
    slots = home_dev * CAP + page_rank
    doc_len = lax.dynamic_index_in_dim(doc_lengths, request, 0, keepdims=False)
    docs = jnp.arange(NDOC)
    doc_start = jnp.sum(jnp.where(docs[None, :] < docs[:, None], doc_len[None, :], 0), axis=1)
    doc_cos, doc_sin = rope_tables(doc_start)
    starts = (doc_start - ctx_rank * S_DEV).astype(jnp.int32)
    blocks = jnp.stack([ctx_rank, (1 - yh) * ZZ + z]).astype(jnp.int32)
    positions = jnp.concatenate([local, local], axis=1)[:, :, None]

    pages = lax.all_to_all(kv_pool[0], CTX, split_axis=0, concat_axis=0, tiled=True)

    x = hidden_rows.reshape(REQ * R, hidden_rows.shape[2])
    x_rank = lax.axis_index("x")
    theirs = partials(jnp.stack([1 - core, x_rank, request]).astype(jnp.int32), x, w_qkv)
    received = lax.ppermute(theirs, "core", [(0, 1), (1, 0)])
    mine = partials(jnp.stack([core, x_rank, request]).astype(jnp.int32), x, w_qkv, received)
    pieces = [mine[0, 0]] + [
        lax.ppermute(mine[far // XX, far % XX], ("yl", "x"), [(j, j ^ far) for j in range(YL * XX)])
        for far in range(1, YL * XX)
    ]
    queries, fresh = make_queries(pieces, query_cos, query_sin)
    queries = lax.all_to_all(
        queries.reshape(NCTX, HALF, HD), CTX, split_axis=0, concat_axis=0, tiled=True
    )

    own = build_block(slots, starts, pages, local_index, fresh, doc_cos, doc_sin)
    other = lax.ppermute(own, "yh", [(0, 1), (1, 0)])
    parts = attend(blocks, queries, own, other, positions)
    parts = lax.all_to_all(parts, CTX, split_axis=0, concat_axis=0, tiled=True)
    return (merge(parts)[None], own[None])


def solution(mesh):
    fine = Mesh(mesh.devices.reshape(YH, ZZ, YL, XX, CC), ("yh", "z", "yl", "x", "core"))
    head = ("yl", "x", "core")
    in_specs = (
        P(None, CTX, head),
        P(None, head, None),
        P(head, CTX, None, None),
        P(),
        P(),
        P(),
    )
    out_specs = (P(head, CTX, None), P(head, CTX, None))
    return jax.shard_map(
        per_device, mesh=fine, in_specs=in_specs, out_specs=out_specs, check_vma=False
    )
```

```python
import functools
import math

import jax
import jax.numpy as jnp
from jax import lax
from jax.experimental import pallas as pl
from jax.experimental.pallas import tpu as pltpu
from jax.sharding import Mesh, PartitionSpec as P

HD = 128
KVH = 8
QG = 4
REQ = 2
PAGE = 128
CAP = 2
S_DEV = 2048
R = 128
NDOC = 8
PAGES_DEV = S_DEV // PAGE

YH, ZZ, YL, XX, CC = 2, 8, 2, 4, 2
CTX = ("yh", "z")
NCTX = YH * ZZ
GROUPS = QG // YH
TILE = 2 * R
TAIL = 16
LOG2E = 1.4426950408889634
SCALE2 = LOG2E / math.sqrt(HD)
EMPTY = -1e30
MIB = 1 << 20

bf16 = jnp.bfloat16
f32 = jnp.float32


def rope_tables(positions):
    half_dim = HD // 2
    inverse = jnp.exp(jnp.arange(half_dim, dtype=f32) * (-2.0 * math.log(500000.0) / HD))
    angles = positions.astype(f32)[:, None] * inverse[None, :]
    cosine, sine = jnp.cos(angles), jnp.sin(angles)
    return (jnp.concatenate([cosine, cosine], axis=1), jnp.concatenate([-sine, sine], axis=1))


def rotated(v, cosine, sine):
    return v * cosine + pltpu.roll(v, HD // 2, 1) * sine


def partial_send_kernel(at_ref, x_ref, w_ref, o_ref):
    acc = jnp.dot(x_ref[...], w_ref[0], preferred_element_type=f32)
    for r in range(REQ):
        o_ref[0, r ^ at_ref[2]] = acc[r * R : (r + 1) * R].astype(bf16)


def partials_to_send(place, x, w):
    d, c = w.shape[1:]
    return pl.pallas_call(
        partial_send_kernel,
        out_shape=jax.ShapeDtypeStruct((XX, REQ, R, c), bf16),
        grid_spec=pltpu.PrefetchScalarGridSpec(
            num_scalar_prefetch=1,
            grid=(XX,),
            in_specs=[
                pl.BlockSpec((REQ * R, d), lambda i, at: (0, 0)),
                pl.BlockSpec((1, d, c), lambda i, at: (2 * (i ^ at[1]) + 1 - at[0], 0, 0)),
            ],
            out_specs=pl.BlockSpec((1, REQ, R, c), lambda i, at: (i, 0, 0, 0)),
        ),
        compiler_params=pltpu.CompilerParams(vmem_limit_bytes=24 * MIB),
    )(place, x, w)


def partial_keep_kernel(at_ref, x_ref, w_ref, r_ref, o_ref):
    acc = jnp.dot(x_ref[...], w_ref[0], preferred_element_type=f32)
    for r in range(REQ):
        far = r ^ at_ref[2]
        o_ref[far] = (acc[r * R : (r + 1) * R] + r_ref[0, far].astype(f32)).astype(bf16)


def partials_to_keep(place, x, w, received, far):
    d, c = w.shape[1:]
    return pl.pallas_call(
        partial_keep_kernel,
        out_shape=jax.ShapeDtypeStruct((REQ, R, c), bf16),
        grid_spec=pltpu.PrefetchScalarGridSpec(
            num_scalar_prefetch=1,
            grid=(1,),
            in_specs=[
                pl.BlockSpec((REQ * R, d), lambda i, at: (0, 0)),
                pl.BlockSpec((1, d, c), lambda i, at: (2 * (far ^ at[1]) + at[0], 0, 0)),
                pl.BlockSpec((1, REQ, R, c), lambda i, at: (far, 0, 0, 0)),
            ],
            out_specs=pl.BlockSpec((REQ, R, c), lambda i, at: (0, 0, 0)),
        ),
        compiler_params=pltpu.CompilerParams(vmem_limit_bytes=24 * MIB),
    )(place, x, w, received)


def gather_kernel(*refs):
    *piece_refs, keep_ref, send_ref = refs
    keep_ref[...] = sum(p_ref[0].astype(f32) for p_ref in piece_refs)
    send_ref[...] = sum(p_ref[1].astype(f32) for p_ref in piece_refs).astype(bf16)


def sum_pieces(pieces):
    c = pieces[0].shape[2]
    whole = pl.BlockSpec(memory_space=pltpu.VMEM)
    return pl.pallas_call(
        gather_kernel,
        out_shape=(jax.ShapeDtypeStruct((R, c), f32), jax.ShapeDtypeStruct((R, c), bf16)),
        in_specs=[whole] * len(pieces),
        out_specs=(whole, whole),
        compiler_params=pltpu.CompilerParams(vmem_limit_bytes=24 * MIB),
    )(*pieces)


def query_kernel(a_ref, b_ref, cos_ref, sin_ref, *out_refs):
    *q_refs, fresh_ref = out_refs
    cosine, sine = cos_ref[...], sin_ref[...]
    total = a_ref[...] + b_ref[...].astype(f32)
    for h in range(QG):
        q = (rotated(total[:, h * HD : (h + 1) * HD], cosine, sine) * SCALE2).astype(bf16)
        for z in range(ZZ):
            q_refs[h % GROUPS][h // GROUPS * ZZ + z] = q
    fresh_ref[:, :HD] = rotated(total[:, QG * HD : (QG + 1) * HD], cosine, sine).astype(bf16)
    fresh_ref[:, HD:] = total[:, (QG + 1) * HD :].astype(bf16)


def make_queries(kept, received, cosine, sine):
    whole = pl.BlockSpec(memory_space=pltpu.VMEM)
    return pl.pallas_call(
        query_kernel,
        out_shape=(
            *[jax.ShapeDtypeStruct((NCTX, R, HD), bf16)] * GROUPS,
            jax.ShapeDtypeStruct((R, 2 * HD), bf16),
        ),
        in_specs=[whole] * 4,
        out_specs=(whole,) * (GROUPS + 1),
        compiler_params=pltpu.CompilerParams(vmem_limit_bytes=24 * MIB),
    )(kept, received, cosine, sine)


def kv_kernel(slot_ref, start_ref, page_ref, idx_ref, fresh_ref, cos_ref, sin_ref, o_ref, x_ref, buf_ref, sem):
    copies = [
        pltpu.make_async_copy(page_ref.at[slot_ref[g]], buf_ref.at[g], sem.at[g])
        for g in range(PAGES_DEV)
    ]
    for copy in copies:
        copy.start()
    column = lax.broadcasted_iota(jnp.int32, (PAGE, HD), 0)
    fresh_rows = jnp.concatenate([fresh_ref[...], jnp.ones((R, HD), bf16)], axis=1)
    for g, copy in enumerate(copies):
        row = column + g * PAGE
        cosine = jnp.broadcast_to(cos_ref[0:1, :], (PAGE, HD))
        sine = jnp.broadcast_to(sin_ref[0:1, :], (PAGE, HD))
        for d in range(1, NDOC):
            later = row >= start_ref[d]
            cosine = jnp.where(later, cos_ref[d : d + 1, :], cosine)
            sine = jnp.where(later, sin_ref[d : d + 1, :], sine)
        hit = jnp.where(idx_ref[...] == row, 1.0, 0.0).astype(bf16)
        fresh = jnp.dot(hit, fresh_rows, preferred_element_type=f32)
        replaced = fresh[:, 2 * HD :] > 0.0
        copy.wait()
        keys = rotated(buf_ref[g, :, :HD].astype(f32), cosine, sine)
        values = buf_ref[g, :, HD:].astype(f32)
        keys = jnp.where(replaced, fresh[:, :HD], keys).astype(bf16)
        values = jnp.where(replaced, fresh[:, HD : 2 * HD], values).astype(bf16)
        here = pl.ds(g * PAGE, PAGE)
        o_ref[here, :HD] = keys
        o_ref[here, HD:] = values
        x_ref[g, :PAGE] = keys
        x_ref[g, PAGE:] = jnp.transpose(values)


def build_block(slots, starts, pages, local_index, fresh, cosine, sine):
    whole = pl.BlockSpec(memory_space=pltpu.VMEM)
    return pl.pallas_call(
        kv_kernel,
        out_shape=(
            jax.ShapeDtypeStruct((S_DEV, 2 * HD), bf16),
            jax.ShapeDtypeStruct((PAGES_DEV, 2 * PAGE, HD), bf16),
        ),
        grid_spec=pltpu.PrefetchScalarGridSpec(
            num_scalar_prefetch=2,
            grid=(),
            in_specs=[pl.BlockSpec(memory_space=pl.ANY), whole, whole, whole, whole],
            out_specs=(whole, whole),
            scratch_shapes=[
                pltpu.VMEM((PAGES_DEV, PAGE, 2 * HD), bf16),
                pltpu.SemaphoreType.DMA((PAGES_DEV,)),
            ],
        ),
        compiler_params=pltpu.CompilerParams(vmem_limit_bytes=24 * MIB),
    )(slots, starts, pages, local_index, fresh, cosine, sine)


def attend_kernel(at_ref, q_ref, own_ref, other_ref, pos_ref, o_ref):
    step_pages = 2
    chunk = step_pages * PAGE
    ones = jnp.ones((TAIL, chunk), bf16)

    def fold(m, block, kv_ref, masked, state):
        q = q_ref[m]
        scores = []
        for k in range(0, PAGES_DEV, step_pages):
            keys = jnp.concatenate([kv_ref[k + n, :PAGE] for n in range(step_pages)], axis=0)
            s = lax.dot_general(keys, q, (((1,), (1,)), ((), ())), preferred_element_type=f32)
            if masked:
                key_pos = lax.broadcasted_iota(jnp.int32, (chunk, TILE), 0) + k * PAGE
                s = jnp.where(key_pos <= pos_ref[m] - block * S_DEV, s, EMPTY)
            scores.append(s)
        tops = [jnp.max(s, axis=0, keepdims=True) for s in scores]
        sums = []
        for n, (s, t) in enumerate(zip(scores, tops)):
            weights = jnp.exp2(s - t).astype(bf16)
            values = jnp.concatenate(
                [kv_ref[n * step_pages + k, PAGE:] for k in range(step_pages)], axis=1
            )
            values = jnp.concatenate([values, ones], axis=0)
            sums.append(jnp.dot(values, weights, preferred_element_type=f32))
        top, total = state
        new_top = functools.reduce(jnp.maximum, tops + [top])
        total = total * jnp.exp2(top - new_top)
        for t, o in zip(tops, sums):
            total = total + o * jnp.exp2(t - new_top)
        return (new_top, total)

    def tile(m, carry):
        first = m * (TILE // R)
        last = first + TILE // R - 1
        state = (jnp.full((1, TILE), EMPTY, f32), jnp.zeros((HD + TAIL, TILE), f32))
        for n, kv_ref in ((1, own_ref), (2, other_ref)):
            block = at_ref[n]
            case = jnp.where(block < first, 2, jnp.where(block <= last, 1, 0))
            state = lax.switch(
                case,
                [
                    lambda s: s,
                    functools.partial(fold, m, block, kv_ref, True),
                    functools.partial(fold, m, block, kv_ref, False),
                ],
                state,
            )
        top, total = state
        denominator = total[HD : HD + 1]
        there = denominator > 0.0
        safe = jnp.where(there, denominator, 1.0)
        result = (total[:HD] / safe).astype(bf16)
        rest = jnp.where(there, top + jnp.log2(safe), EMPTY)
        place = lax.broadcasted_iota(jnp.int32, (TAIL, TILE), 0)
        tail = jnp.zeros((TAIL, TILE), f32)
        for k in range(3):
            term = rest.astype(bf16).astype(f32)
            rest = rest - term
            tail = jnp.where(place == k, term, tail)
        tail = tail.astype(bf16)
        for n in range(TILE // R):
            o_ref[first + n, :HD] = result[:, n * R : (n + 1) * R]
            o_ref[first + n, HD:] = tail[:, n * R : (n + 1) * R]
        return carry

    lax.fori_loop(0, NCTX * R // TILE, tile, 0)


def attend(place, queries, own, other, positions):
    whole = pl.BlockSpec(memory_space=pltpu.VMEM)
    return pl.pallas_call(
        attend_kernel,
        out_shape=jax.ShapeDtypeStruct((NCTX, HD + TAIL, R), bf16),
        grid_spec=pltpu.PrefetchScalarGridSpec(
            num_scalar_prefetch=1, grid=(), in_specs=[whole] * 4, out_specs=whole
        ),
        compiler_params=pltpu.CompilerParams(vmem_limit_bytes=40 * MIB),
    )(place, queries.reshape(NCTX * R // TILE, TILE, HD), own, other, positions)


def merge_kernel(*refs):
    *part_refs, o_ref = refs
    for group, p_ref in enumerate(part_refs):
        for y in range(YH):
            at = range(y * ZZ, (y + 1) * ZZ)
            lse = [sum(p_ref[i, HD + k : HD + k + 1, :].astype(f32) for k in range(3)) for i in at]
            top = functools.reduce(jnp.maximum, lse)
            share = [jnp.exp2(t - top) for t in lse]
            total = sum(p_ref[i, :HD, :].astype(f32) * u for i, u in zip(at, share)) / sum(share)
            head = y * GROUPS + group
            o_ref[:, head * HD : (head + 1) * HD] = jnp.transpose(total).astype(bf16)


def merge(parts):
    whole = pl.BlockSpec(memory_space=pltpu.VMEM)
    return pl.pallas_call(
        merge_kernel,
        out_shape=jax.ShapeDtypeStruct((R, QG * HD), bf16),
        in_specs=[whole] * len(parts),
        out_specs=whole,
        compiler_params=pltpu.CompilerParams(vmem_limit_bytes=24 * MIB),
    )(*parts)


def per_device(hidden_rows, w_qkv, kv_pool, page_home, recompute_idx, doc_lengths):
    yh, z = lax.axis_index("yh"), lax.axis_index("z")
    request = lax.axis_index("yl")
    core = lax.axis_index("core")
    ctx_rank = yh * ZZ + z

    local = lax.dynamic_index_in_dim(recompute_idx.reshape(REQ, NCTX, R), request, 0, False)
    local_index = lax.dynamic_slice(local, (ctx_rank, 0), (1, R))
    query_cos, query_sin = rope_tables(ctx_rank * S_DEV + local_index[0])
    home_dev = lax.dynamic_slice(
        page_home, (request, ctx_rank * PAGES_DEV, 0), (1, PAGES_DEV, 1)
    ).reshape(PAGES_DEV)
    same_home = home_dev[:, None] == home_dev[None, :]
    earlier = jnp.arange(PAGES_DEV)[:, None] > jnp.arange(PAGES_DEV)[None, :]
    page_rank = jnp.sum(jnp.where(same_home & earlier, 1, 0), axis=1).astype(jnp.int32)
    slots = home_dev * CAP + page_rank
    doc_len = lax.dynamic_index_in_dim(doc_lengths, request, 0, keepdims=False)
    docs = jnp.arange(NDOC)
    doc_start = jnp.sum(jnp.where(docs[None, :] < docs[:, None], doc_len[None, :], 0), axis=1)
    doc_cos, doc_sin = rope_tables(doc_start)
    starts = (doc_start - ctx_rank * S_DEV).astype(jnp.int32)
    place = jnp.stack([yh, ctx_rank, (1 - yh) * ZZ + z]).astype(jnp.int32)
    positions = (local + jnp.arange(NCTX, dtype=jnp.int32)[:, None] * S_DEV).reshape(
        NCTX * R // TILE, 1, TILE
    )

    pages = lax.all_to_all(kv_pool[0], CTX, split_axis=0, concat_axis=0, tiled=True)

    x = hidden_rows.reshape(REQ * R, hidden_rows.shape[2])
    w = pltpu.with_memory_space_constraint(w_qkv, pltpu.HBM)
    x_rank = lax.axis_index("x")
    corner = jnp.stack([core, x_rank, request]).astype(jnp.int32)
    swap = [(0, 1), (1, 0)]
    received = lax.ppermute(partials_to_send(corner, x, w), "core", swap)
    pieces = []
    for far in (2, 1, 3, 0):
        mine = partials_to_keep(corner, x, w, received, far)
        if far:
            mine = lax.ppermute(mine, "x", [(j, j ^ far) for j in range(XX)])
        pieces.append(mine)
    kept, handed = sum_pieces(pieces)
    *queries, fresh = make_queries(kept, lax.ppermute(handed, "yl", swap), query_cos, query_sin)
    queries = [lax.all_to_all(q, CTX, split_axis=0, concat_axis=0, tiled=True) for q in queries]

    own, packed = build_block(slots, starts, pages, local_index, fresh, doc_cos, doc_sin)
    other = lax.ppermute(packed, "yh", swap)
    parts = [
        lax.all_to_all(
            attend(place, q, packed, other, positions), CTX, split_axis=0, concat_axis=0, tiled=True
        )
        for q in queries
    ]
    return (merge(parts)[None], own[None])


def solution(mesh):
    fine = Mesh(mesh.devices.reshape(YH, ZZ, YL, XX, CC), ("yh", "z", "yl", "x", "core"))
    head = ("yl", "x", "core")
    in_specs = (
        P(None, CTX, head),
        P(None, head, None),
        P(head, CTX, None, None),
        P(),
        P(),
        P(),
    )
    out_specs = (P(head, CTX, None), P(head, CTX, None))
    return jax.shard_map(
        per_device, mesh=fine, in_specs=in_specs, out_specs=out_specs, check_vma=False
    )
```

```python
import functools
import math

import jax
import jax.numpy as jnp
from jax import lax
from jax.experimental import pallas as pl
from jax.experimental.pallas import tpu as pltpu
from jax.sharding import Mesh, PartitionSpec as P

HD = 128
KVH = 8
QG = 4
REQ = 2
PAGE = 128
CAP = 2
S_DEV = 2048
R = 128
NDOC = 8
PAGES_DEV = S_DEV // PAGE

YH, ZZ, YL, XX, CC = 2, 8, 2, 4, 2
CTX = ("yh", "z")
NCTX = YH * ZZ
GROUPS = QG // YH
TILE = GROUPS * R
TAIL = 16
LOG2E = 1.4426950408889634
SCALE2 = LOG2E / math.sqrt(HD)
EMPTY = -1e30
MIB = 1 << 20

bf16 = jnp.bfloat16
f32 = jnp.float32


def rope_tables(positions):
    half_dim = HD // 2
    inverse = jnp.exp(jnp.arange(half_dim, dtype=f32) * (-2.0 * math.log(500000.0) / HD))
    angles = positions.astype(f32)[:, None] * inverse[None, :]
    cosine, sine = jnp.cos(angles), jnp.sin(angles)
    return (jnp.concatenate([cosine, cosine], axis=1), jnp.concatenate([-sine, sine], axis=1))


def rotated(v, cosine, sine):
    return v * cosine + pltpu.roll(v, HD // 2, 1) * sine


def partial_send_kernel(at_ref, x_ref, w_ref, o_ref):
    acc = jnp.dot(x_ref[...], w_ref[0], preferred_element_type=f32)
    for r in range(REQ):
        o_ref[0, r ^ at_ref[2]] = acc[r * R : (r + 1) * R].astype(bf16)


def partials_to_send(place, x, w):
    d, c = w.shape[1:]
    return pl.pallas_call(
        partial_send_kernel,
        out_shape=jax.ShapeDtypeStruct((XX, REQ, R, c), bf16),
        grid_spec=pltpu.PrefetchScalarGridSpec(
            num_scalar_prefetch=1,
            grid=(XX,),
            in_specs=[
                pl.BlockSpec((REQ * R, d), lambda i, at: (0, 0)),
                pl.BlockSpec((1, d, c), lambda i, at: (2 * (i ^ at[1]) + 1 - at[0], 0, 0)),
            ],
            out_specs=pl.BlockSpec((1, REQ, R, c), lambda i, at: (i, 0, 0, 0)),
        ),
        compiler_params=pltpu.CompilerParams(vmem_limit_bytes=24 * MIB),
    )(place, x, w)


def partial_keep_kernel(at_ref, x_ref, w_ref, r_ref, o_ref):
    acc = jnp.dot(x_ref[...], w_ref[0], preferred_element_type=f32)
    for r in range(REQ):
        far = r ^ at_ref[2]
        o_ref[far] = (acc[r * R : (r + 1) * R] + r_ref[0, far].astype(f32)).astype(bf16)


def partials_to_keep(place, x, w, received, far):
    d, c = w.shape[1:]
    return pl.pallas_call(
        partial_keep_kernel,
        out_shape=jax.ShapeDtypeStruct((REQ, R, c), bf16),
        grid_spec=pltpu.PrefetchScalarGridSpec(
            num_scalar_prefetch=1,
            grid=(1,),
            in_specs=[
                pl.BlockSpec((REQ * R, d), lambda i, at: (0, 0)),
                pl.BlockSpec((1, d, c), lambda i, at: (2 * (far ^ at[1]) + at[0], 0, 0)),
                pl.BlockSpec((1, REQ, R, c), lambda i, at: (far, 0, 0, 0)),
            ],
            out_specs=pl.BlockSpec((REQ, R, c), lambda i, at: (0, 0, 0)),
        ),
        compiler_params=pltpu.CompilerParams(vmem_limit_bytes=24 * MIB),
    )(place, x, w, received)


def gather_kernel(*refs):
    *piece_refs, keep_ref, send_ref = refs
    keep_ref[...] = sum(p_ref[0].astype(f32) for p_ref in piece_refs)
    send_ref[...] = sum(p_ref[1].astype(f32) for p_ref in piece_refs).astype(bf16)


def sum_pieces(pieces):
    c = pieces[0].shape[2]
    whole = pl.BlockSpec(memory_space=pltpu.VMEM)
    return pl.pallas_call(
        gather_kernel,
        out_shape=(jax.ShapeDtypeStruct((R, c), f32), jax.ShapeDtypeStruct((R, c), bf16)),
        in_specs=[whole] * len(pieces),
        out_specs=(whole, whole),
        compiler_params=pltpu.CompilerParams(vmem_limit_bytes=24 * MIB),
    )(*pieces)


def query_kernel(at_ref, a_ref, b_ref, cos_ref, sin_ref, mine_ref, theirs_ref, fresh_ref):
    cosine, sine = cos_ref[...], sin_ref[...]
    total = a_ref[...] + b_ref[...].astype(f32)
    for y in range(YH):
        for n in range(GROUPS):
            h = y * GROUPS + n
            q = (rotated(total[:, h * HD : (h + 1) * HD], cosine, sine) * SCALE2).astype(bf16)

            @pl.when(at_ref[0] == y)
            def _():
                mine_ref[n * R : (n + 1) * R] = q

            @pl.when(at_ref[0] != y)
            def _():
                theirs_ref[n * R : (n + 1) * R] = q

    fresh_ref[:, :HD] = rotated(total[:, QG * HD : (QG + 1) * HD], cosine, sine).astype(bf16)
    fresh_ref[:, HD:] = total[:, (QG + 1) * HD :].astype(bf16)


def make_queries(place, kept, received, cosine, sine):
    whole = pl.BlockSpec(memory_space=pltpu.VMEM)
    half = jax.ShapeDtypeStruct((TILE, HD), bf16)
    return pl.pallas_call(
        query_kernel,
        out_shape=(half, half, jax.ShapeDtypeStruct((R, 2 * HD), bf16)),
        grid_spec=pltpu.PrefetchScalarGridSpec(
            num_scalar_prefetch=1, grid=(), in_specs=[whole] * 4, out_specs=(whole,) * 3
        ),
        compiler_params=pltpu.CompilerParams(vmem_limit_bytes=24 * MIB),
    )(place, kept, received, cosine, sine)


def kv_kernel(slot_ref, start_ref, page_ref, idx_ref, fresh_ref, cos_ref, sin_ref, o_ref, x_ref, buf_ref, sem):
    copies = [
        pltpu.make_async_copy(page_ref.at[slot_ref[g]], buf_ref.at[g], sem.at[g])
        for g in range(PAGES_DEV)
    ]
    for copy in copies:
        copy.start()
    column = lax.broadcasted_iota(jnp.int32, (PAGE, HD), 0)
    fresh_rows = jnp.concatenate([fresh_ref[...], jnp.ones((R, HD), bf16)], axis=1)
    for g, copy in enumerate(copies):
        row = column + g * PAGE
        cosine = jnp.broadcast_to(cos_ref[0:1, :], (PAGE, HD))
        sine = jnp.broadcast_to(sin_ref[0:1, :], (PAGE, HD))
        for d in range(1, NDOC):
            later = row >= start_ref[d]
            cosine = jnp.where(later, cos_ref[d : d + 1, :], cosine)
            sine = jnp.where(later, sin_ref[d : d + 1, :], sine)
        hit = jnp.where(idx_ref[...] == row, 1.0, 0.0).astype(bf16)
        fresh = jnp.dot(hit, fresh_rows, preferred_element_type=f32)
        replaced = fresh[:, 2 * HD :] > 0.0
        copy.wait()
        keys = rotated(buf_ref[g, :, :HD].astype(f32), cosine, sine)
        values = buf_ref[g, :, HD:].astype(f32)
        keys = jnp.where(replaced, fresh[:, :HD], keys).astype(bf16)
        values = jnp.where(replaced, fresh[:, HD : 2 * HD], values).astype(bf16)
        here = pl.ds(g * PAGE, PAGE)
        o_ref[here, :HD] = keys
        o_ref[here, HD:] = values
        x_ref[g, :PAGE] = keys
        x_ref[g, PAGE:] = jnp.transpose(values)


def build_block(slots, starts, pages, local_index, fresh, cosine, sine):
    whole = pl.BlockSpec(memory_space=pltpu.VMEM)
    return pl.pallas_call(
        kv_kernel,
        out_shape=(
            jax.ShapeDtypeStruct((S_DEV, 2 * HD), bf16),
            jax.ShapeDtypeStruct((PAGES_DEV, 2 * PAGE, HD), bf16),
        ),
        grid_spec=pltpu.PrefetchScalarGridSpec(
            num_scalar_prefetch=2,
            grid=(),
            in_specs=[pl.BlockSpec(memory_space=pl.ANY), whole, whole, whole, whole],
            out_specs=(whole, whole),
            scratch_shapes=[
                pltpu.VMEM((PAGES_DEV, PAGE, 2 * HD), bf16),
                pltpu.SemaphoreType.DMA((PAGES_DEV,)),
            ],
        ),
        compiler_params=pltpu.CompilerParams(vmem_limit_bytes=24 * MIB),
    )(slots, starts, pages, local_index, fresh, cosine, sine)


def attend_kernel(at_ref, q_ref, own_ref, other_ref, pos_ref, o_ref):
    step_pages = 2
    chunk = step_pages * PAGE
    ones = jnp.ones((TAIL, chunk), bf16)

    def fold(c, kv_ref, masked, state):
        q = q_ref[c % ZZ, (c // ZZ) ^ at_ref[0]]
        scores = []
        for k in range(0, PAGES_DEV, step_pages):
            keys = jnp.concatenate([kv_ref[k + n, :PAGE] for n in range(step_pages)], axis=0)
            s = lax.dot_general(keys, q, (((1,), (1,)), ((), ())), preferred_element_type=f32)
            if masked:
                key_pos = lax.broadcasted_iota(jnp.int32, (chunk, TILE), 0) + k * PAGE
                s = jnp.where(key_pos <= pos_ref[c], s, EMPTY)
            scores.append(s)
        tops = [jnp.max(s, axis=0, keepdims=True) for s in scores]
        sums = []
        for n, (s, t) in enumerate(zip(scores, tops)):
            weights = jnp.exp2(s - t).astype(bf16)
            values = jnp.concatenate(
                [kv_ref[n * step_pages + k, PAGE:] for k in range(step_pages)], axis=1
            )
            values = jnp.concatenate([values, ones], axis=0)
            sums.append(jnp.dot(values, weights, preferred_element_type=f32))
        top, total = state
        new_top = functools.reduce(jnp.maximum, tops + [top])
        total = total * jnp.exp2(top - new_top)
        for t, o in zip(tops, sums):
            total = total + o * jnp.exp2(t - new_top)
        return (new_top, total)

    def tile(c, carry):
        state = (jnp.full((1, TILE), EMPTY, f32), jnp.zeros((HD + TAIL, TILE), f32))
        for n, kv_ref in ((1, own_ref), (2, other_ref)):
            block = at_ref[n]
            case = jnp.where(block < c, 2, jnp.where(block == c, 1, 0))
            state = lax.switch(
                case,
                [
                    lambda s: s,
                    functools.partial(fold, c, kv_ref, True),
                    functools.partial(fold, c, kv_ref, False),
                ],
                state,
            )
        top, total = state
        denominator = total[HD : HD + 1]
        there = denominator > 0.0
        safe = jnp.where(there, denominator, 1.0)
        o_ref[c, :HD] = (total[:HD] / safe).astype(bf16)
        rest = jnp.where(there, top + jnp.log2(safe), EMPTY)
        place = lax.broadcasted_iota(jnp.int32, (TAIL, TILE), 0)
        tail = jnp.zeros((TAIL, TILE), f32)
        for k in range(3):
            term = rest.astype(bf16).astype(f32)
            rest = rest - term
            tail = jnp.where(place == k, term, tail)
        o_ref[c, HD:] = tail.astype(bf16)
        return carry

    lax.fori_loop(0, NCTX, tile, 0)


def attend(place, queries, own, other, positions):
    whole = pl.BlockSpec(memory_space=pltpu.VMEM)
    return pl.pallas_call(
        attend_kernel,
        out_shape=jax.ShapeDtypeStruct((NCTX, HD + TAIL, TILE), bf16),
        grid_spec=pltpu.PrefetchScalarGridSpec(
            num_scalar_prefetch=1, grid=(), in_specs=[whole] * 4, out_specs=whole
        ),
        compiler_params=pltpu.CompilerParams(vmem_limit_bytes=40 * MIB),
    )(place, queries, own, other, positions)


def merge_kernel(p_ref, o_ref):
    for y in range(YH):
        at = range(y * ZZ, (y + 1) * ZZ)
        lse = [sum(p_ref[i, HD + k : HD + k + 1, :].astype(f32) for k in range(3)) for i in at]
        top = functools.reduce(jnp.maximum, lse)
        share = [jnp.exp2(t - top) for t in lse]
        total = sum(p_ref[i, :HD, :].astype(f32) * u for i, u in zip(at, share)) / sum(share)
        for n in range(GROUPS):
            h = y * GROUPS + n
            o_ref[:, h * HD : (h + 1) * HD] = jnp.transpose(total[:, n * R : (n + 1) * R]).astype(bf16)


def merge(parts):
    whole = pl.BlockSpec(memory_space=pltpu.VMEM)
    return pl.pallas_call(
        merge_kernel,
        out_shape=jax.ShapeDtypeStruct((R, QG * HD), bf16),
        in_specs=[whole],
        out_specs=whole,
        compiler_params=pltpu.CompilerParams(vmem_limit_bytes=24 * MIB),
    )(parts)


def per_device(hidden_rows, w_qkv, kv_pool, page_home, recompute_idx, doc_lengths):
    yh, z = lax.axis_index("yh"), lax.axis_index("z")
    request = lax.axis_index("yl")
    core = lax.axis_index("core")
    ctx_rank = yh * ZZ + z

    local = lax.dynamic_index_in_dim(recompute_idx.reshape(REQ, NCTX, R), request, 0, False)
    local_index = lax.dynamic_slice(local, (ctx_rank, 0), (1, R))
    query_cos, query_sin = rope_tables(ctx_rank * S_DEV + local_index[0])
    home_dev = lax.dynamic_slice(
        page_home, (request, ctx_rank * PAGES_DEV, 0), (1, PAGES_DEV, 1)
    ).reshape(PAGES_DEV)
    same_home = home_dev[:, None] == home_dev[None, :]
    earlier = jnp.arange(PAGES_DEV)[:, None] > jnp.arange(PAGES_DEV)[None, :]
    page_rank = jnp.sum(jnp.where(same_home & earlier, 1, 0), axis=1).astype(jnp.int32)
    slots = home_dev * CAP + page_rank
    doc_len = lax.dynamic_index_in_dim(doc_lengths, request, 0, keepdims=False)
    docs = jnp.arange(NDOC)
    doc_start = jnp.sum(jnp.where(docs[None, :] < docs[:, None], doc_len[None, :], 0), axis=1)
    doc_cos, doc_sin = rope_tables(doc_start)
    starts = (doc_start - ctx_rank * S_DEV).astype(jnp.int32)
    place = jnp.stack([yh, ctx_rank, (1 - yh) * ZZ + z]).astype(jnp.int32)
    positions = jnp.concatenate([local] * GROUPS, axis=1)[:, None, :]

    pages = lax.all_to_all(kv_pool[0], CTX, split_axis=0, concat_axis=0, tiled=True)

    x = hidden_rows.reshape(REQ * R, hidden_rows.shape[2])
    w = pltpu.with_memory_space_constraint(w_qkv, pltpu.HBM)
    x_rank = lax.axis_index("x")
    corner = jnp.stack([core, x_rank, request]).astype(jnp.int32)
    swap = [(0, 1), (1, 0)]
    received = lax.ppermute(partials_to_send(corner, x, w), "core", swap)
    pieces = []
    for far in (2, 1, 3, 0):
        mine = partials_to_keep(corner, x, w, received, far)
        if far:
            mine = lax.ppermute(mine, "x", [(j, j ^ far) for j in range(XX)])
        pieces.append(mine)
    kept, handed = sum_pieces(pieces)
    mine, theirs, fresh = make_queries(
        place, kept, lax.ppermute(handed, "yl", swap), query_cos, query_sin
    )
    halves = jnp.stack([mine, lax.ppermute(theirs, "yh", swap)])
    queries = lax.all_to_all(
        jnp.broadcast_to(halves[None], (ZZ, YH, TILE, HD)), "z", split_axis=0, concat_axis=0, tiled=True
    )

    own, packed = build_block(slots, starts, pages, local_index, fresh, doc_cos, doc_sin)
    other = lax.ppermute(packed, "yh", swap)
    parts = attend(place, queries, packed, other, positions)
    parts = lax.all_to_all(parts, CTX, split_axis=0, concat_axis=0, tiled=True)
    return (merge(parts)[None], own[None])


def solution(mesh):
    fine = Mesh(mesh.devices.reshape(YH, ZZ, YL, XX, CC), ("yh", "z", "yl", "x", "core"))
    head = ("yl", "x", "core")
    in_specs = (
        P(None, CTX, head),
        P(None, head, None),
        P(head, CTX, None, None),
        P(),
        P(),
        P(),
    )
    out_specs = (P(head, CTX, None), P(head, CTX, None))
    return jax.shard_map(
        per_device, mesh=fine, in_specs=in_specs, out_specs=out_specs, check_vma=False
    )
```

```python
import functools
import math

import jax
import jax.numpy as jnp
from jax import lax
from jax.experimental import pallas as pl
from jax.experimental.pallas import tpu as pltpu
from jax.sharding import Mesh, PartitionSpec as P

HD = 128
KVH = 8
QG = 4
REQ = 2
PAGE = 128
CAP = 2
S_DEV = 2048
R = 128
NDOC = 8
PAGES_DEV = S_DEV // PAGE

YH, ZZ, YL, XX, CC = 2, 8, 2, 4, 2
CTX = ("yh", "z")
NCTX = YH * ZZ
GROUPS = QG // YH
TILE = GROUPS * R
TAIL = 8
LOG2E = 1.4426950408889634
SCALE2 = LOG2E / math.sqrt(HD)
EMPTY = -1e30
MIB = 1 << 20

bf16 = jnp.bfloat16
f32 = jnp.float32


def rope_tables(positions):
    half_dim = HD // 2
    inverse = jnp.exp(jnp.arange(half_dim, dtype=f32) * (-2.0 * math.log(500000.0) / HD))
    angles = positions.astype(f32)[:, None] * inverse[None, :]
    cosine, sine = jnp.cos(angles), jnp.sin(angles)
    return (jnp.concatenate([cosine, cosine], axis=1), jnp.concatenate([-sine, sine], axis=1))


def rotated(v, cosine, sine):
    return v * cosine + pltpu.roll(v, HD // 2, 1) * sine


def partial_send_kernel(at_ref, x_ref, w_ref, o_ref):
    acc = jnp.dot(x_ref[...], w_ref[0], preferred_element_type=f32)
    for r in range(REQ):
        o_ref[0, r ^ at_ref[2]] = acc[r * R : (r + 1) * R].astype(bf16)


def partials_to_send(place, x, w):
    d, c = w.shape[1:]
    return pl.pallas_call(
        partial_send_kernel,
        out_shape=jax.ShapeDtypeStruct((XX, REQ, R, c), bf16),
        grid_spec=pltpu.PrefetchScalarGridSpec(
            num_scalar_prefetch=1,
            grid=(XX,),
            in_specs=[
                pl.BlockSpec((REQ * R, d), lambda i, at: (0, 0)),
                pl.BlockSpec((1, d, c), lambda i, at: (2 * (i ^ at[1]) + 1 - at[0], 0, 0)),
            ],
            out_specs=pl.BlockSpec((1, REQ, R, c), lambda i, at: (i, 0, 0, 0)),
        ),
        compiler_params=pltpu.CompilerParams(vmem_limit_bytes=24 * MIB),
    )(place, x, w)


def partial_keep_kernel(at_ref, x_ref, w_ref, r_ref, o_ref):
    acc = jnp.dot(x_ref[...], w_ref[0], preferred_element_type=f32)
    for r in range(REQ):
        far = r ^ at_ref[2]
        o_ref[far] = (acc[r * R : (r + 1) * R] + r_ref[0, far].astype(f32)).astype(bf16)


def partials_to_keep(place, x, w, received, far):
    d, c = w.shape[1:]
    return pl.pallas_call(
        partial_keep_kernel,
        out_shape=jax.ShapeDtypeStruct((REQ, R, c), bf16),
        grid_spec=pltpu.PrefetchScalarGridSpec(
            num_scalar_prefetch=1,
            grid=(1,),
            in_specs=[
                pl.BlockSpec((REQ * R, d), lambda i, at: (0, 0)),
                pl.BlockSpec((1, d, c), lambda i, at: (2 * (far ^ at[1]) + at[0], 0, 0)),
                pl.BlockSpec((1, REQ, R, c), lambda i, at: (far, 0, 0, 0)),
            ],
            out_specs=pl.BlockSpec((REQ, R, c), lambda i, at: (0, 0, 0)),
        ),
        compiler_params=pltpu.CompilerParams(vmem_limit_bytes=24 * MIB),
    )(place, x, w, received)


def gather_kernel(*refs):
    *piece_refs, keep_ref, send_ref = refs
    keep_ref[...] = sum(p_ref[0].astype(f32) for p_ref in piece_refs)
    send_ref[...] = sum(p_ref[1].astype(f32) for p_ref in piece_refs).astype(bf16)


def sum_pieces(pieces):
    c = pieces[0].shape[2]
    whole = pl.BlockSpec(memory_space=pltpu.VMEM)
    return pl.pallas_call(
        gather_kernel,
        out_shape=(jax.ShapeDtypeStruct((R, c), f32), jax.ShapeDtypeStruct((R, c), bf16)),
        in_specs=[whole] * len(pieces),
        out_specs=(whole, whole),
        compiler_params=pltpu.CompilerParams(vmem_limit_bytes=24 * MIB),
    )(*pieces)


def query_kernel(at_ref, a_ref, b_ref, cos_ref, sin_ref, mine_ref, theirs_ref, fresh_ref):
    cosine, sine = cos_ref[...], sin_ref[...]
    total = a_ref[...] + b_ref[...].astype(f32)
    for y in range(YH):
        for n in range(GROUPS):
            h = y * GROUPS + n
            q = (rotated(total[:, h * HD : (h + 1) * HD], cosine, sine) * SCALE2).astype(bf16)

            @pl.when(at_ref[0] == y)
            def _():
                mine_ref[n * R : (n + 1) * R] = q

            @pl.when(at_ref[0] != y)
            def _():
                theirs_ref[n * R : (n + 1) * R] = q

    fresh_ref[:, :HD] = rotated(total[:, QG * HD : (QG + 1) * HD], cosine, sine).astype(bf16)
    fresh_ref[:, HD:] = total[:, (QG + 1) * HD :].astype(bf16)


def make_queries(place, kept, received, cosine, sine):
    whole = pl.BlockSpec(memory_space=pltpu.VMEM)
    half = jax.ShapeDtypeStruct((TILE, HD), bf16)
    return pl.pallas_call(
        query_kernel,
        out_shape=(half, half, jax.ShapeDtypeStruct((R, 2 * HD), bf16)),
        grid_spec=pltpu.PrefetchScalarGridSpec(
            num_scalar_prefetch=1, grid=(), in_specs=[whole] * 4, out_specs=(whole,) * 3
        ),
        compiler_params=pltpu.CompilerParams(vmem_limit_bytes=24 * MIB),
    )(place, kept, received, cosine, sine)


def kv_kernel(
    slot_ref, start_ref, page_ref, idx_ref, fresh_ref, cos_ref, sin_ref, mine_ref, theirs_ref,
    o_ref, x_ref, q_ref, buf_ref, sem,
):
    copies = [
        pltpu.make_async_copy(page_ref.at[slot_ref[g]], buf_ref.at[g], sem.at[g])
        for g in range(PAGES_DEV)
    ]
    for copy in copies:
        copy.start()
    q_ref[0] = mine_ref[...]
    q_ref[1] = theirs_ref[...]
    column = lax.broadcasted_iota(jnp.int32, (PAGE, HD), 0)
    fresh_rows = jnp.concatenate([fresh_ref[...], jnp.ones((R, HD), bf16)], axis=1)
    for g, copy in enumerate(copies):
        row = column + g * PAGE
        cosine = jnp.broadcast_to(cos_ref[0:1, :], (PAGE, HD))
        sine = jnp.broadcast_to(sin_ref[0:1, :], (PAGE, HD))
        for d in range(1, NDOC):
            later = row >= start_ref[d]
            cosine = jnp.where(later, cos_ref[d : d + 1, :], cosine)
            sine = jnp.where(later, sin_ref[d : d + 1, :], sine)
        hit = jnp.where(idx_ref[...] == row, 1.0, 0.0).astype(bf16)
        fresh = jnp.dot(hit, fresh_rows, preferred_element_type=f32)
        replaced = fresh[:, 2 * HD :] > 0.0
        copy.wait()
        keys = rotated(buf_ref[g, :, :HD].astype(f32), cosine, sine)
        values = buf_ref[g, :, HD:].astype(f32)
        keys = jnp.where(replaced, fresh[:, :HD], keys).astype(bf16)
        values = jnp.where(replaced, fresh[:, HD : 2 * HD], values).astype(bf16)
        here = pl.ds(g * PAGE, PAGE)
        o_ref[here, :HD] = keys
        o_ref[here, HD:] = values
        x_ref[g, :PAGE] = keys
        x_ref[g, PAGE:] = jnp.transpose(values)


def build_block(slots, starts, pages, local_index, fresh, cosine, sine, mine, theirs):
    whole = pl.BlockSpec(memory_space=pltpu.VMEM)
    return pl.pallas_call(
        kv_kernel,
        out_shape=(
            jax.ShapeDtypeStruct((S_DEV, 2 * HD), bf16),
            jax.ShapeDtypeStruct((PAGES_DEV, 2 * PAGE, HD), bf16),
            jax.ShapeDtypeStruct((YH, TILE, HD), bf16),
        ),
        grid_spec=pltpu.PrefetchScalarGridSpec(
            num_scalar_prefetch=2,
            grid=(),
            in_specs=[pl.BlockSpec(memory_space=pl.ANY), *[whole] * 6],
            out_specs=(whole, whole, whole),
            scratch_shapes=[
                pltpu.VMEM((PAGES_DEV, PAGE, 2 * HD), bf16),
                pltpu.SemaphoreType.DMA((PAGES_DEV,)),
            ],
        ),
        compiler_params=pltpu.CompilerParams(vmem_limit_bytes=24 * MIB),
    )(slots, starts, pages, local_index, fresh, cosine, sine, mine, theirs)


def attend_kernel(at_ref, own_ref, other_ref, pos_ref, *refs):
    *piece_refs, o_ref, q_ref = refs
    for far, piece_ref in enumerate(piece_refs):
        q_ref[at_ref[3] ^ far] = piece_ref[...]
    step_pages = 2
    chunk = step_pages * PAGE
    ones = jnp.ones((TAIL, chunk), bf16)

    def fold(c, kv_refs, masked, state):
        q = q_ref[c % ZZ, (c // ZZ) ^ at_ref[0]]
        units = [(kv_ref, k) for kv_ref in kv_refs for k in range(0, PAGES_DEV, step_pages)]
        scores = []
        for kv_ref, k in units:
            keys = jnp.concatenate([kv_ref[k + n, :PAGE] for n in range(step_pages)], axis=0)
            s = lax.dot_general(keys, q, (((1,), (1,)), ((), ())), preferred_element_type=f32)
            if masked:
                key_pos = lax.broadcasted_iota(jnp.int32, (chunk, TILE), 0) + k * PAGE
                s = jnp.where(key_pos <= pos_ref[c], s, EMPTY)
            scores.append(s)
        tops = [jnp.max(s, axis=0, keepdims=True) for s in scores]
        sums = []
        for (kv_ref, k), s, t in zip(units, scores, tops):
            weights = jnp.exp2(s - t).astype(bf16)
            values = jnp.concatenate([kv_ref[k + n, PAGE:] for n in range(step_pages)], axis=1)
            values = jnp.concatenate([values, ones], axis=0)
            sums.append(jnp.dot(values, weights, preferred_element_type=f32))
        top, total = state
        new_top = functools.reduce(jnp.maximum, tops + [top])
        total = total * jnp.exp2(top - new_top)
        for t, o in zip(tops, sums):
            total = total + o * jnp.exp2(t - new_top)
        return (new_top, total)

    def one_by_one(c, state):
        for n, kv_ref in ((1, own_ref), (2, other_ref)):
            block = at_ref[n]
            case = jnp.where(block < c, 2, jnp.where(block == c, 1, 0))
            state = lax.switch(
                case,
                [
                    lambda s: s,
                    functools.partial(fold, c, [kv_ref], True),
                    functools.partial(fold, c, [kv_ref], False),
                ],
                state,
            )
        return state

    def tile(c, carry):
        state = (jnp.full((1, TILE), EMPTY, f32), jnp.zeros((HD + TAIL, TILE), f32))
        state = lax.cond(
            jnp.maximum(at_ref[1], at_ref[2]) < c,
            functools.partial(fold, c, [own_ref, other_ref], False),
            functools.partial(one_by_one, c),
            state,
        )
        top, total = state
        denominator = total[HD : HD + 1]
        there = denominator > 0.0
        safe = jnp.where(there, denominator, 1.0)
        o_ref[c, :HD] = (total[:HD] / safe).astype(bf16)
        rest = jnp.where(there, top + jnp.log2(safe), EMPTY)
        place = lax.broadcasted_iota(jnp.int32, (TAIL, TILE), 0)
        tail = jnp.zeros((TAIL, TILE), f32)
        for k in range(3):
            term = rest.astype(bf16).astype(f32)
            rest = rest - term
            tail = jnp.where(place == k, term, tail)
        o_ref[c, HD:] = tail.astype(bf16)
        return carry

    lax.fori_loop(0, NCTX, tile, 0)


def attend(place, own, other, positions, queries):
    whole = pl.BlockSpec(memory_space=pltpu.VMEM)
    return pl.pallas_call(
        attend_kernel,
        out_shape=jax.ShapeDtypeStruct((NCTX, HD + TAIL, TILE), bf16),
        grid_spec=pltpu.PrefetchScalarGridSpec(
            num_scalar_prefetch=1,
            grid=(),
            in_specs=[whole] * (3 + len(queries)),
            out_specs=whole,
            scratch_shapes=[pltpu.VMEM((ZZ, YH, TILE, HD), bf16)],
        ),
        compiler_params=pltpu.CompilerParams(vmem_limit_bytes=40 * MIB),
    )(place, own, other, positions, *queries)


def merge_kernel(p_ref, o_ref):
    for y in range(YH):
        at = range(y * ZZ, (y + 1) * ZZ)
        lse = [sum(p_ref[i, HD + k : HD + k + 1, :].astype(f32) for k in range(3)) for i in at]
        top = functools.reduce(jnp.maximum, lse)
        share = [jnp.exp2(t - top) for t in lse]
        total = sum(p_ref[i, :HD, :].astype(f32) * u for i, u in zip(at, share)) / sum(share)
        for n in range(GROUPS):
            h = y * GROUPS + n
            o_ref[:, h * HD : (h + 1) * HD] = jnp.transpose(total[:, n * R : (n + 1) * R]).astype(bf16)


def merge(parts):
    whole = pl.BlockSpec(memory_space=pltpu.VMEM)
    return pl.pallas_call(
        merge_kernel,
        out_shape=jax.ShapeDtypeStruct((R, QG * HD), bf16),
        in_specs=[whole],
        out_specs=whole,
        compiler_params=pltpu.CompilerParams(vmem_limit_bytes=24 * MIB),
    )(parts)


def per_device(hidden_rows, w_qkv, kv_pool, page_home, recompute_idx, doc_lengths):
    yh, z = lax.axis_index("yh"), lax.axis_index("z")
    request = lax.axis_index("yl")
    core = lax.axis_index("core")
    ctx_rank = yh * ZZ + z

    local = lax.dynamic_index_in_dim(recompute_idx.reshape(REQ, NCTX, R), request, 0, False)
    local_index = lax.dynamic_slice(local, (ctx_rank, 0), (1, R))
    query_cos, query_sin = rope_tables(ctx_rank * S_DEV + local_index[0])
    home_dev = lax.dynamic_slice(
        page_home, (request, ctx_rank * PAGES_DEV, 0), (1, PAGES_DEV, 1)
    ).reshape(PAGES_DEV)
    same_home = home_dev[:, None] == home_dev[None, :]
    earlier = jnp.arange(PAGES_DEV)[:, None] > jnp.arange(PAGES_DEV)[None, :]
    page_rank = jnp.sum(jnp.where(same_home & earlier, 1, 0), axis=1).astype(jnp.int32)
    slots = home_dev * CAP + page_rank
    doc_len = lax.dynamic_index_in_dim(doc_lengths, request, 0, keepdims=False)
    docs = jnp.arange(NDOC)
    doc_start = jnp.sum(jnp.where(docs[None, :] < docs[:, None], doc_len[None, :], 0), axis=1)
    doc_cos, doc_sin = rope_tables(doc_start)
    starts = (doc_start - ctx_rank * S_DEV).astype(jnp.int32)
    place = jnp.stack([yh, ctx_rank, (1 - yh) * ZZ + z, z]).astype(jnp.int32)
    positions = jnp.concatenate([local] * GROUPS, axis=1)[:, None, :]

    pages = lax.all_to_all(kv_pool[0], CTX, split_axis=0, concat_axis=0, tiled=True)

    x = hidden_rows.reshape(REQ * R, hidden_rows.shape[2])
    w = pltpu.with_memory_space_constraint(w_qkv, pltpu.HBM)
    x_rank = lax.axis_index("x")
    corner = jnp.stack([core, x_rank, request]).astype(jnp.int32)
    swap = [(0, 1), (1, 0)]
    received = lax.ppermute(partials_to_send(corner, x, w), "core", swap)
    pieces = []
    for far in (2, 1, 3, 0):
        mine = partials_to_keep(corner, x, w, received, far)
        if far:
            mine = lax.ppermute(mine, "x", [(j, j ^ far) for j in range(XX)])
        pieces.append(mine)
    kept, handed = sum_pieces(pieces)
    mine, theirs, fresh = make_queries(
        place, kept, lax.ppermute(handed, "yl", swap), query_cos, query_sin
    )
    own, packed, halves = build_block(
        slots, starts, pages, local_index, fresh, doc_cos, doc_sin, mine, lax.ppermute(theirs, "yh", swap)
    )
    other = lax.ppermute(packed, "yh", swap)
    queries = [halves] + [
        lax.ppermute(halves, "z", [(j, j ^ far) for j in range(ZZ)]) for far in range(1, ZZ)
    ]
    parts = attend(place, packed, other, positions, queries)
    parts = lax.all_to_all(parts, CTX, split_axis=0, concat_axis=0, tiled=True)
    return (merge(parts)[None], own[None])


def solution(mesh):
    fine = Mesh(mesh.devices.reshape(YH, ZZ, YL, XX, CC), ("yh", "z", "yl", "x", "core"))
    head = ("yl", "x", "core")
    in_specs = (
        P(None, CTX, head),
        P(None, head, None),
        P(head, CTX, None, None),
        P(),
        P(),
        P(),
    )
    out_specs = (P(head, CTX, None), P(head, CTX, None))
    return jax.shard_map(
        per_device, mesh=fine, in_specs=in_specs, out_specs=out_specs, check_vma=False
    )
```
